32 devices in a mesh: beam: 2 (over y), sub: 8 (over z, x), tm: 2 (over core).
Axes of the slice: x: 2, y: 2, z: 4, core: 2. Of those that a mesh axis runs over, the one named last changes fastest.
Arguments:
- filterbank: bfloat16 [2048, 1024], P(('beam', 'sub'), 'tm'), parts along dimension 0, may hold values from -6 to 6
- bandpass: float32 [2048], P(('beam', 'sub')), parts along dimension 0, may hold values from 0.3 to 3
- local_delays: int32 [7, 1024], P(None, 'sub'), may hold values from 0 to 32, as said below
- cross_delays: int32 [3, 128], P(None, 'sub'), may hold values from 0 to 32, as said below
Outputs:
- dedispersed: float32 [256, 1024], P(('beam', 'sub'), 'tm'), parts along dimension 0
The draws below stay inside these ranges and needn't reach their ends.
There are 2 independent parts, one for each index of `beam`. The reference program is written for one: setup_inputs(seed, part) draws one part's arguments, and reference() takes and returns one part's arrays. A program takes and returns all parts, laid end to end along the dimension named above; an argument that names none is the same for every part. Nothing has to cross between parts.
Inputs may be any that keep to these rules, and one draw needn't show every extreme that they name: `local_delays`: whole samples; level m of the local levels reads its first entries of each block of 128. `cross_delays`: whole samples.
All inputs are finite; a program needn't handle non-finite values.
Results may differ from the reference program's by a relative error of at most 0.0003.
Values may be sent and summed in bfloat16 or wider, within the bound.
A program may use at most 64 MiB of HBM per device.

```python
import math
import jax
import jax.numpy as jnp
from jax import lax

CH_DEV = 128
KD = 16
CHANNELS = 1024
SAMPLES = 1024
TRIALS = 128
LLEV = 7
XLEV = 3
SHIFT_MAX = 32
N_SUB = 8


def draw_local_delays(key, part):
    delays = jax.random.randint(key, (LLEV, CHANNELS), 0, SHIFT_MAX + 1, dtype=jnp.int32)
    return delays.at[0, 0].set(SHIFT_MAX)


def draw_cross_delays(key, part):
    delays = jax.random.randint(jax.random.fold_in(key, 7), (XLEV, TRIALS), 0, SHIFT_MAX + 1, dtype=jnp.int32)
    return delays.at[XLEV - 1, 0].set(SHIFT_MAX)


def level_of(own_key, dims, pieces, least, top_value):
    level, own = 1.0, jax.random.fold_in(own_key, 6)
    for axis_at, parts in pieces:
        draws = jnp.exp(jax.random.uniform(jax.random.fold_in(own, axis_at), (parts,), jnp.float32, least / len(pieces), top_value / len(pieces)))
        level = level * jnp.repeat(draws, dims[axis_at] // parts).reshape([-1 if axis == axis_at else 1 for axis in range(len(dims))])
    return level


def scatter_about(own_key, shape, width, bound, split=(), kind=jnp.bfloat16):
    factor_of = level_of(own_key, shape, split, -0.22, 0.18) if split else 1.0
    array = jax.random.normal(own_key, shape, jnp.float32) * width * factor_of
    return jnp.minimum(jnp.maximum(array, -bound), bound).astype(kind)


def setup_inputs(seed: int = 0, part: int = 0) -> dict:
    streams_of = jax.random.split(jax.random.key(seed), 5)
    own_keys = jax.random.split(jax.random.fold_in(streams_of[4], part), 5)
    filterbank = scatter_about(own_keys[0], (CHANNELS, SAMPLES), 1.0, 6.0, ((0, 8), (1, 2)))
    bandpass = jnp.clip(jnp.exp(math.log(3.0) - 2.3025851 * jax.random.uniform(own_keys[1], (CHANNELS,), jnp.float32) ** level_of(own_keys[1], (CHANNELS,), ((0, 8),), -0.2, 0.2)), 0.3, 3.0)
    local_delays = draw_local_delays(jax.random.fold_in(streams_of[4], 71), part)
    cross_delays = draw_cross_delays(jax.random.fold_in(streams_of[4], 71), part)
    return dict(filterbank=filterbank, bandpass=bandpass, local_delays=local_delays, cross_delays=cross_delays)


def delayed(upper, delays):
    padded = jnp.pad(upper, ((0, 0), (SHIFT_MAX, 0)))
    columns = lax.broadcasted_iota(jnp.int32, upper.shape, 1)
    offsets = columns + SHIFT_MAX - delays[:, None].astype(jnp.int32)
    return jnp.take_along_axis(padded, offsets, axis=1)

def reference(filterbank, bandpass, local_delays, cross_delays):
    corrected = filterbank.astype(jnp.float32) * bandpass[:, None]
    padded = jnp.pad(corrected, ((0, 0), (15, 15)))
    window_total = lax.reduce_window(padded, jnp.zeros((), padded.dtype), lax.add, (1, 31), (1, 1), 'VALID')
    current = corrected - window_total / 31.0
    trial_count = 1
    for level_index in range(LLEV):
        band_count = current.shape[0] // trial_count
        grouped = current.reshape(band_count // 2, 2, trial_count, SAMPLES)
        lower = grouped[:, 0]
        upper = grouped[:, 1]
        new_count = min(2 * trial_count, KD)
        if new_count > trial_count:
            lower = jnp.concatenate([lower, lower], axis=1)
            upper = jnp.concatenate([upper, upper], axis=1)
        per_device = band_count // 2 // N_SUB * new_count
        delays = local_delays[level_index].reshape(N_SUB, CH_DEV)[:, :per_device].reshape(-1)
        current = lower.reshape(-1, SAMPLES) + delayed(upper.reshape(-1, SAMPLES), delays)
        trial_count = new_count
    for level_index in range(XLEV):
        grouped = current.reshape(-1, 2, trial_count, SAMPLES)
        lower = jnp.concatenate([grouped[:, 0], grouped[:, 0]], axis=1)
        upper = jnp.concatenate([grouped[:, 1], grouped[:, 1]], axis=1)
        current = lower.reshape(-1, SAMPLES) + delayed(upper.reshape(-1, SAMPLES), cross_delays[level_index])
        trial_count = 2 * trial_count
    return current * (1.0 / math.sqrt(CHANNELS))
```

```python
import functools
import math

import jax
import jax.numpy as jnp
from jax import lax
from jax.experimental import pallas as pl
from jax.experimental.pallas import tpu as pltpu
from jax.sharding import PartitionSpec as P

MESH = pl.DeviceIdType.MESH
LANES = 128
SUB = 8
HALF = 15
WINDOW = 31.0


def tiles_of(columns):
    return -(-columns // LANES)


def delayed(tiles, delay, lane, count):
    tiles = tiles[max(0, len(tiles) - count - 1) :]
    source = (lane - delay) & (LANES - 1)
    keep = lane >= delay
    turned = [jnp.take_along_axis(t, source, axis=1, mode="promise_in_bounds") for t in tiles]
    if len(turned) == count:
        turned = [jnp.zeros_like(turned[0])] + turned
    return [jnp.where(keep, turned[k + 1], turned[k]) for k in range(count)]


def kernel(
    geometry,
    fb_hbm, bp_hbm, ld_hbm, cd_hbm,
    out_ref,
    fpad, bp_v, ld_v, cd_v, x0, delay_l, delay_c, plane, sent, got,
    load_sem, halo_send, halo_recv, cross_send, cross_recv,
):
    channels, span, local_levels, cross_levels, trials, shift_max, norm = geometry
    own = span // LANES
    reach = (local_levels + cross_levels) * shift_max
    halo = tiles_of(reach + HALF)
    growth = trials.bit_length() - 1
    row_tiles = trials // SUB
    tm = lax.axis_index("tm")
    sub = lax.axis_index("sub")
    other = 1 - tm

    barrier = pltpu.get_barrier_semaphore()
    pl.semaphore_signal(barrier, inc=1, device_id={"tm": other}, device_id_type=MESH)
    for level in range(cross_levels):
        pl.semaphore_signal(barrier, inc=1, device_id={"sub": sub ^ (1 << level)}, device_id_type=MESH)

    first, last = halo * LANES, (halo + own) * LANES
    loads = [
        pltpu.make_async_copy(ld_hbm, ld_v, load_sem.at[0]),
        pltpu.make_async_copy(cd_hbm, cd_v, load_sem.at[1]),
        pltpu.make_async_copy(bp_hbm, bp_v, load_sem.at[2]),
        pltpu.make_async_copy(fb_hbm, fpad.at[:, first:last], load_sem.at[3]),
    ]
    for load in loads:
        load.start()

    @pl.when(tm == 0)
    def _():
        fpad[:, :first] = jnp.zeros((channels, first), fpad.dtype)

    @pl.when(tm == 1)
    def _():
        fpad[:, last:] = jnp.zeros((channels, LANES), fpad.dtype)

    pl.semaphore_wait(barrier, 1 + cross_levels)
    ahead = pltpu.make_async_remote_copy(
        src_ref=fb_hbm.at[:, span - first :], dst_ref=fpad.at[:, :first],
        send_sem=halo_send.at[0], recv_sem=halo_recv.at[0],
        device_id={"tm": other}, device_id_type=MESH,
    )
    back = pltpu.make_async_remote_copy(
        src_ref=fb_hbm.at[:, :LANES], dst_ref=fpad.at[:, last:],
        send_sem=halo_send.at[1], recv_sem=halo_recv.at[1],
        device_id={"tm": other}, device_id_type=MESH,
    )

    @pl.when(tm == 0)
    def _():
        ahead.start()

    @pl.when(tm == 1)
    def _():
        back.start()

    for load in loads[:3]:
        load.wait()
    ones = jnp.ones((channels, LANES), jnp.float32).astype(jnp.bfloat16)
    row_at = lax.broadcasted_iota(jnp.int32, (channels, channels), 0)
    col_at = lax.broadcasted_iota(jnp.int32, (channels, channels), 1)
    diagonal = row_at == col_at
    rows = channels
    for level in range(local_levels):
        if level >= growth:
            rows //= 2
        spread = jnp.where(diagonal[:rows], ld_v[level : level + 1, :].astype(jnp.float32), 0.0)
        spread = jnp.dot(spread.astype(jnp.bfloat16), ones, preferred_element_type=jnp.float32)
        delay_l[level, :rows, :] = spread.astype(jnp.int32)
    for level in range(cross_levels):
        spread = jnp.where(diagonal[:trials, :trials], cd_v[level : level + 1, :].astype(jnp.float32), 0.0)
        spread = jnp.dot(spread.astype(jnp.bfloat16), ones[:trials], preferred_element_type=jnp.float32)
        delay_c[level] = spread.astype(jnp.int32)
    gain = jnp.dot(
        jnp.where(diagonal, bp_v[...], 0.0), jnp.ones((channels, LANES), jnp.float32),
        precision=lax.Precision.HIGHEST, preferred_element_type=jnp.float32,
    )
    halo_gain = gain * tm.astype(jnp.float32)
    band_row = lax.broadcasted_iota(jnp.int32, (3 * LANES, LANES), 0)
    band_col = lax.broadcasted_iota(jnp.int32, (3 * LANES, LANES), 1)
    apart = band_row - LANES - band_col
    band = jnp.where((apart >= -HALF) & (apart <= HALF), 1.0, 0.0).astype(jnp.bfloat16)

    loads[3].wait()

    @pl.when(tm == 0)
    def _():
        ahead.wait_send()
        back.wait_recv()

    @pl.when(tm == 1)
    def _():
        back.wait_send()
        ahead.wait_recv()

    for k in range(halo + own):
        low = max(k - 1, 0)
        total = jnp.dot(
            fpad[:, low * LANES : (k + 2) * LANES], band[(low - k + 1) * LANES :],
            preferred_element_type=jnp.float32,
        )
        centre = fpad[:, k * LANES : (k + 1) * LANES].astype(jnp.float32)
        x0[:, k * LANES : (k + 1) * LANES] = (halo_gain if k < halo else gain) * (centre - total / WINDOW)

    lane = lax.broadcasted_iota(jnp.int32, (SUB, LANES), 1)
    sublane = lax.broadcasted_iota(jnp.int32, (SUB, LANES), 0)
    counts = [own + tiles_of(reach - (m + 1) * shift_max) for m in range(local_levels + cross_levels)]

    def block(at, carry):
        base = at * trials
        current = []
        for r in range(row_tiles):
            here = pl.ds(pl.multiple_of(base + r * SUB, SUB), SUB)
            current.append([x0[here, k * LANES : (k + 1) * LANES] for k in range(halo + own)])
        for level in range(growth):
            count, step = counts[level], 1 << level
            following = []
            for r in range(row_tiles):
                delay = delay_l[level, pl.ds(pl.multiple_of(base + r * SUB, SUB), SUB), :]
                if step < SUB:
                    is_upper = (sublane & step) != 0
                    lower, upper = [], []
                    for t in current[r]:
                        down = pltpu.roll(t, step, 0)
                        up = down if 2 * step == SUB else pltpu.roll(t, SUB - step, 0)
                        lower.append(jnp.where(is_upper, down, t))
                        upper.append(jnp.where(is_upper, t, up))
                else:
                    apart = step // SUB
                    lower, upper = current[r & ~apart], current[r | apart]
                moved = delayed(upper, delay, lane, count)
                following.append([a + b for a, b in zip(lower[len(lower) - count :], moved)])
            current = following
        for r in range(row_tiles):
            here = pl.ds(pl.multiple_of(base + r * SUB, SUB), SUB)
            for k, t in enumerate(current[r]):
                plane[here, k * LANES : (k + 1) * LANES] = t
        return carry

    lax.fori_loop(0, channels // trials, block, 0)

    bands = channels // trials
    count = counts[growth - 1]
    current = [
        [[plane[(b * row_tiles + r) * SUB : (b * row_tiles + r + 1) * SUB, k * LANES : (k + 1) * LANES] for k in range(count)] for r in range(row_tiles)]
        for b in range(bands)
    ]
    for level in range(growth, local_levels):
        count = counts[level]
        bands //= 2
        following = []
        for b in range(bands):
            made = []
            for r in range(row_tiles):
                at = (b * row_tiles + r) * SUB
                moved = delayed(current[2 * b + 1][r], delay_l[level, at : at + SUB, :], lane, count)
                lower = current[2 * b][r]
                made.append([x + y for x, y in zip(lower[len(lower) - count :], moved)])
            following.append(made)
        current = following
    rows_of = current[0]

    def exchange(level, r, skip):
        here = (level, pl.ds(r * SUB, SUB), pl.ds(skip * LANES, (width - skip) * LANES))
        return pltpu.make_async_remote_copy(
            src_ref=sent.at[here], dst_ref=got.at[here],
            send_sem=cross_send.at[level, r], recv_sem=cross_recv.at[level, r],
            device_id={"sub": sub ^ (1 << level)}, device_id_type=MESH,
        )

    width = len(rows_of[0])
    copies = []

    def send(level, r):
        skip = width - len(rows_of[r])
        for k, t in enumerate(rows_of[r], skip):
            sent[level, r * SUB : (r + 1) * SUB, k * LANES : (k + 1) * LANES] = t
        copy = exchange(level, r, skip)
        copy.start()
        copies.append(copy)
        return copy

    flight = [send(0, r) for r in range(row_tiles)] if cross_levels else []
    for level in range(cross_levels):
        count = counts[local_levels + level]
        on_top = (sub >> level) & 1 == 1
        for r in range(row_tiles):
            mine = rows_of[r]
            flight[r].wait_recv()
            skip = width - len(mine)
            theirs = [got[level, r * SUB : (r + 1) * SUB, (k + skip) * LANES : (k + skip + 1) * LANES] for k in range(len(mine))]
            lower = [jnp.where(on_top, t, m) for t, m in zip(theirs, mine)]
            upper = [jnp.where(on_top, m, t) for t, m in zip(theirs, mine)]
            moved = delayed(upper, delay_c[level, r * SUB : (r + 1) * SUB, :], lane, count)
            rows_of[r] = [x + y for x, y in zip(lower[len(lower) - count :], moved)]
            if level + 1 < cross_levels:
                flight[r] = send(level + 1, r)
    for r in range(row_tiles):
        for k, t in enumerate(rows_of[r][-own:]):
            out_ref[r * SUB : (r + 1) * SUB, k * LANES : (k + 1) * LANES] = t * norm
    for copy in copies:
        copy.wait_send()


def shards(filterbank, bandpass, local_delays, cross_delays):
    channels, span = filterbank.shape
    shift_max = span // 16
    local_levels = local_delays.shape[0]
    cross_levels = lax.axis_size("sub").bit_length() - 1
    trials = cross_delays.shape[1]
    norm = 1.0 / math.sqrt(channels * lax.axis_size("sub"))
    own = span // LANES
    reach = (local_levels + cross_levels) * shift_max
    halo = tiles_of(reach + HALF)
    width = (own + tiles_of(cross_levels * shift_max)) * LANES
    geometry = (channels, span, local_levels, cross_levels, trials, shift_max, norm)
    return pl.pallas_call(
        functools.partial(kernel, geometry),
        out_shape=jax.ShapeDtypeStruct((trials, span), jnp.float32),
        in_specs=[pl.BlockSpec(memory_space=pl.ANY)] * 4,
        out_specs=pl.BlockSpec(memory_space=pltpu.VMEM),
        scratch_shapes=[
            pltpu.VMEM((channels, (halo + own + 1) * LANES), jnp.bfloat16),
            pltpu.VMEM((1, channels), jnp.float32),
            pltpu.VMEM(local_delays.shape, jnp.int32),
            pltpu.VMEM(cross_delays.shape, jnp.int32),
            pltpu.VMEM((channels, (halo + own) * LANES), jnp.float32),
            pltpu.VMEM((local_levels, channels, LANES), jnp.int32),
            pltpu.VMEM((max(cross_levels, 1), trials, LANES), jnp.int32),
            pltpu.VMEM((channels, (halo + own) * LANES), jnp.float32),
            pltpu.VMEM((max(cross_levels, 1), trials, width), jnp.float32),
            pltpu.VMEM((max(cross_levels, 1), trials, width), jnp.float32),
            pltpu.SemaphoreType.DMA((4,)),
            pltpu.SemaphoreType.DMA((2,)),
            pltpu.SemaphoreType.DMA((2,)),
            pltpu.SemaphoreType.DMA((max(cross_levels, 1), trials // SUB)),
            pltpu.SemaphoreType.DMA((max(cross_levels, 1), trials // SUB)),
        ],
        compiler_params=pltpu.CompilerParams(collective_id=0, has_side_effects=True),
    )(filterbank, bandpass.reshape(1, channels), local_delays, cross_delays)


def solution(mesh):
    return jax.shard_map(
        shards,
        mesh=mesh,
        in_specs=(P(("beam", "sub"), "tm"), P(("beam", "sub")), P(None, "sub"), P(None, "sub")),
        out_specs=P(("beam", "sub"), "tm"),
        check_vma=False,
    )
```

```python
import functools
import math

import jax
import jax.numpy as jnp
from jax import lax
from jax.experimental import pallas as pl
from jax.experimental.pallas import tpu as pltpu
from jax.sharding import PartitionSpec as P

MESH = pl.DeviceIdType.MESH
LANES = 128
SUB = 8
HALF = 15
WINDOW = 31.0


def tiles_of(columns):
    return -(-columns // LANES)


def delayed(tiles, delay, lane, count):
    tiles = tiles[max(0, len(tiles) - count - 1) :]
    source = (lane - delay) & (LANES - 1)
    keep = lane >= delay
    turned = [jnp.take_along_axis(t, source, axis=1, mode="promise_in_bounds") for t in tiles]
    if len(turned) == count:
        turned = [jnp.zeros_like(turned[0])] + turned
    return [jnp.where(keep, turned[k + 1], turned[k]) for k in range(count)]


def merged_right(lower, upper, delay, lane, count):
    source = (lane - delay) & (LANES - 1)
    keep = lane >= delay
    turned = [jnp.take_along_axis(t, source, axis=1, mode="promise_in_bounds") for t in upper]
    zero = jnp.zeros_like(turned[0])
    made = []
    for k in range(count):
        here = turned[k] if k < len(turned) else zero
        left = turned[k - 1] if k else zero
        moved = jnp.where(keep, here, left)
        made.append(lower[k] + moved if k < len(lower) else moved)
    return made


def paired(mine, theirs, on_top, delay, lane, count):
    lower = [jnp.where(on_top, t, m) for t, m in zip(theirs, mine)]
    upper = [jnp.where(on_top, m, t) for t, m in zip(theirs, mine)]
    moved = delayed(upper, delay, lane, count)
    return [a + b for a, b in zip(lower[len(lower) - count :], moved)]


def phases_of(cross_levels):
    phases = []
    for level in range(0, cross_levels, 2):
        one = 1 << level
        phases.append((level, (one, 2 * one, 3 * one) if level + 1 < cross_levels else (one,)))
    return phases


def kernel(
    geometry,
    fb_hbm, bp_hbm, ld_hbm, cd_hbm,
    out_ref,
    fpad, bp_v, ld_v, cd_v, x0, delay_l, delay_c, delay_far, plane, edge_sent, edge_got, sent, got,
    load_sem, edge_send, edge_recv, far_send, far_recv, cross_send, cross_recv,
):
    channels, span, local_levels, cross_levels, trials, shift_max, norm = geometry
    own = span // LANES
    before = tiles_of(cross_levels * shift_max)
    width = before + own
    growth = trials.bit_length() - 1
    row_tiles = trials // SUB
    tm = lax.axis_index("tm")
    sub = lax.axis_index("sub")
    other = 1 - tm
    phases = phases_of(cross_levels)

    barrier = pltpu.get_barrier_semaphore()
    pl.semaphore_signal(barrier, inc=1, device_id={"tm": other}, device_id_type=MESH)
    partners = 1
    for level, masks in phases:
        for mask in masks:
            pl.semaphore_signal(barrier, inc=1, device_id={"sub": sub ^ mask}, device_id_type=MESH)
            partners += 1

    counts = [tiles_of(span + HALF + (m + 1) * shift_max) for m in range(local_levels)]
    start = own + 1
    loads = [
        pltpu.make_async_copy(ld_hbm, ld_v, load_sem.at[0]),
        pltpu.make_async_copy(cd_hbm, cd_v, load_sem.at[1]),
        pltpu.make_async_copy(bp_hbm, bp_v, load_sem.at[2]),
        pltpu.make_async_copy(
            fb_hbm, fpad.at[:, pl.ds(pl.multiple_of(tm * LANES, LANES), span)], load_sem.at[3]
        ),
    ]
    for load in loads:
        load.start()

    @pl.when(tm == 0)
    def _():
        fpad[:, span : start * LANES] = jnp.zeros((channels, LANES), fpad.dtype)
        edge_got[:, : (width - 1) * LANES] = jnp.zeros((trials, (width - 1) * LANES), jnp.float32)

    edge_tiles = counts[-1] - own + before

    @pl.when(tm == 1)
    def _():
        fpad[:, :LANES] = jnp.zeros((channels, LANES), fpad.dtype)
        if edge_tiles < width:
            edge_got[:, edge_tiles * LANES :] = jnp.zeros((trials, (width - edge_tiles) * LANES), jnp.float32)

    for load in loads[:3]:
        load.wait()
    ones = jnp.ones((channels, LANES), jnp.float32).astype(jnp.bfloat16)
    row_at = lax.broadcasted_iota(jnp.int32, (channels, channels), 0)
    col_at = lax.broadcasted_iota(jnp.int32, (channels, channels), 1)
    diagonal = row_at == col_at
    rows = channels
    for level in range(local_levels):
        if level >= growth:
            rows //= 2
        spread = jnp.where(diagonal[:rows], ld_v[level : level + 1, :].astype(jnp.float32), 0.0)
        spread = jnp.dot(spread.astype(jnp.bfloat16), ones, preferred_element_type=jnp.float32)
        delay_l[level, :rows, :] = spread.astype(jnp.int32)
    for level in range(cross_levels):
        spread = jnp.where(diagonal[:trials, :trials], cd_v[level : level + 1, :].astype(jnp.float32), 0.0)
        spread = jnp.dot(spread.astype(jnp.bfloat16), ones[:trials], preferred_element_type=jnp.float32)
        delay_c[level] = spread.astype(jnp.int32)
    gain = jnp.dot(
        jnp.where(diagonal, bp_v[...], 0.0), jnp.ones((channels, LANES), jnp.float32),
        precision=lax.Precision.HIGHEST, preferred_element_type=jnp.float32,
    )
    band_row = lax.broadcasted_iota(jnp.int32, (3 * LANES, LANES), 0)
    band_col = lax.broadcasted_iota(jnp.int32, (3 * LANES, LANES), 1)
    apart = band_row - LANES - band_col
    band = jnp.where((apart >= -HALF) & (apart <= HALF), 1.0, 0.0).astype(jnp.bfloat16)

    loads[3].wait()
    for k in range(start):
        low, high = max(k - 1, 0), min(k + 2, start)
        total = jnp.dot(
            fpad[:, low * LANES : high * LANES], band[(low - k + 1) * LANES : (high - k + 1) * LANES],
            preferred_element_type=jnp.float32,
        )
        centre = fpad[:, k * LANES : (k + 1) * LANES].astype(jnp.float32)
        x0[:, k * LANES : (k + 1) * LANES] = gain * (centre - total / WINDOW)

    lane = lax.broadcasted_iota(jnp.int32, (SUB, LANES), 1)
    sublane = lax.broadcasted_iota(jnp.int32, (SUB, LANES), 0)

    def block(at, carry):
        base = at * trials
        current = []
        for r in range(row_tiles):
            here = pl.ds(pl.multiple_of(base + r * SUB, SUB), SUB)
            current.append([x0[here, k * LANES : (k + 1) * LANES] for k in range(start)])
        for level in range(growth):
            count, step = counts[level], 1 << level
            following = []
            for r in range(row_tiles):
                delay = delay_l[level, pl.ds(pl.multiple_of(base + r * SUB, SUB), SUB), :]
                if step < SUB:
                    is_upper = (sublane & step) != 0
                    lower, upper = [], []
                    for t in current[r]:
                        down = pltpu.roll(t, step, 0)
                        up = down if 2 * step == SUB else pltpu.roll(t, SUB - step, 0)
                        lower.append(jnp.where(is_upper, down, t))
                        upper.append(jnp.where(is_upper, t, up))
                else:
                    apart = step // SUB
                    lower, upper = current[r & ~apart], current[r | apart]
                following.append(merged_right(lower, upper, delay, lane, count))
            current = following
        for r in range(row_tiles):
            here = pl.ds(pl.multiple_of(base + r * SUB, SUB), SUB)
            for k, t in enumerate(current[r]):
                plane[here, k * LANES : (k + 1) * LANES] = t
        return carry

    lax.fori_loop(0, channels // trials, block, 0)

    bands = channels // trials
    count = counts[growth - 1]
    current = [
        [[plane[(b * row_tiles + r) * SUB : (b * row_tiles + r + 1) * SUB, k * LANES : (k + 1) * LANES] for k in range(count)] for r in range(row_tiles)]
        for b in range(bands)
    ]
    for level in range(growth, local_levels):
        count = counts[level]
        bands //= 2
        following = []
        for b in range(bands):
            made = []
            for r in range(row_tiles):
                at = (b * row_tiles + r) * SUB
                delay = delay_l[level, at : at + SUB, :]
                made.append(merged_right(current[2 * b][r], current[2 * b + 1][r], delay, lane, count))
            following.append(made)
        current = following
    frame = current[0]

    for r in range(row_tiles):
        for k, t in enumerate(frame[r]):
            edge_sent[r * SUB : (r + 1) * SUB, k * LANES : (k + 1) * LANES] = t
    pl.semaphore_wait(barrier, partners)

    far_copies = []
    for at, (level, masks) in enumerate(phases):
        if len(masks) > 1:
            copy = pltpu.make_async_remote_copy(
                src_ref=delay_c.at[level], dst_ref=delay_far.at[at],
                send_sem=far_send.at[at], recv_sem=far_recv.at[at],
                device_id={"sub": sub ^ masks[1]}, device_id_type=MESH,
            )
            far_copies.append(copy)

    def edges(r):
        here = pl.ds(r * SUB, SUB)
        onward = pltpu.make_async_remote_copy(
            src_ref=edge_sent.at[here, pl.ds((own - before) * LANES, edge_tiles * LANES)],
            dst_ref=edge_got.at[here, pl.ds(0, edge_tiles * LANES)],
            send_sem=edge_send.at[0, r], recv_sem=edge_recv.at[0, r],
            device_id={"tm": other}, device_id_type=MESH,
        )
        backward = pltpu.make_async_remote_copy(
            src_ref=edge_sent.at[here, pl.ds(0, LANES)],
            dst_ref=edge_got.at[here, pl.ds((width - 1) * LANES, LANES)],
            send_sem=edge_send.at[1, r], recv_sem=edge_recv.at[1, r],
            device_id={"tm": other}, device_id_type=MESH,
        )
        return onward, backward

    edge_copies = [edges(r) for r in range(row_tiles)]

    @pl.when(tm == 0)
    def _():
        for onward, backward in edge_copies:
            onward.start()

    @pl.when(tm == 1)
    def _():
        for onward, backward in edge_copies:
            backward.start()

    for copy in far_copies:
        copy.start()

    copies = []

    def send(at, r, tiles):
        skip = width - len(tiles)
        for k, t in enumerate(tiles, skip):
            sent[at, r * SUB : (r + 1) * SUB, k * LANES : (k + 1) * LANES] = t
        made = []
        for slot, mask in enumerate(phases[at][1]):
            copy = pltpu.make_async_remote_copy(
                src_ref=sent.at[at, pl.ds(r * SUB, SUB), pl.ds(skip * LANES, len(tiles) * LANES)],
                dst_ref=got.at[at, slot, pl.ds(r * SUB, SUB), pl.ds(skip * LANES, len(tiles) * LANES)],
                send_sem=cross_send.at[at, slot, r], recv_sem=cross_recv.at[at, slot, r],
                device_id={"sub": sub ^ mask}, device_id_type=MESH,
            )
            copy.start()
            made.append(copy)
        copies.extend(made)
        return made

    rows_of, flight = [], []
    for r in range(row_tiles):
        onward, backward = edge_copies[r]

        @pl.when(tm == 0)
        def _():
            backward.wait_recv()

        @pl.when(tm == 1)
        def _():
            onward.wait_recv()

        tiles = []
        for t in range(-before, own):
            k = t + before
            piece = edge_got[r * SUB : (r + 1) * SUB, k * LANES : (k + 1) * LANES]
            zero = jnp.zeros_like(piece)
            early = frame[r][t] if t >= 0 else zero
            late = frame[r][t + 1] if t >= -1 else zero
            tiles.append(piece + jnp.where(tm == 1, late, early))
        rows_of.append(tiles)
        if phases:
            flight.append(send(0, r, tiles))

    for at, (level, masks) in enumerate(phases):
        if len(masks) > 1:
            far_copies[[a for a, p in enumerate(phases) if len(p[1]) > 1].index(at)].wait_recv()
        for r in range(row_tiles):
            mine = rows_of[r]
            here = slice(r * SUB, (r + 1) * SUB)
            skip = width - len(mine)

            def landed(slot):
                flight[r][slot].wait_recv()
                return [got[at, slot, here, (k + skip) * LANES : (k + skip + 1) * LANES] for k in range(len(mine))]

            made = paired(mine, landed(0), (sub >> level) & 1 == 1, delay_c[level, here, :], lane, own + tiles_of((cross_levels - level - 1) * shift_max))
            if len(masks) > 1:
                far = paired(landed(1), landed(2), (sub >> level) & 1 == 1, delay_far[at, here, :], lane, len(made))
                made = paired(made, far, (sub >> (level + 1)) & 1 == 1, delay_c[level + 1, here, :], lane, own + tiles_of((cross_levels - level - 2) * shift_max))
            rows_of[r] = made
            if at + 1 < len(phases):
                flight[r] = send(at + 1, r, made)
    for r in range(row_tiles):
        for k, t in enumerate(rows_of[r][-own:]):
            out_ref[r * SUB : (r + 1) * SUB, k * LANES : (k + 1) * LANES] = t * norm
    for copy in copies + far_copies:
        copy.wait_send()

    @pl.when(tm == 0)
    def _():
        for onward, backward in edge_copies:
            onward.wait_send()

    @pl.when(tm == 1)
    def _():
        for onward, backward in edge_copies:
            backward.wait_send()


def shards(filterbank, bandpass, local_delays, cross_delays):
    channels, span = filterbank.shape
    shift_max = span // 16
    local_levels = local_delays.shape[0]
    cross_levels = lax.axis_size("sub").bit_length() - 1
    trials = cross_delays.shape[1]
    norm = 1.0 / math.sqrt(channels * lax.axis_size("sub"))
    own = span // LANES
    width = (own + tiles_of(cross_levels * shift_max)) * LANES
    frame = tiles_of(span + HALF + local_levels * shift_max) * LANES
    phases = max(len(phases_of(cross_levels)), 1)
    row_tiles = trials // SUB
    geometry = (channels, span, local_levels, cross_levels, trials, shift_max, norm)
    return pl.pallas_call(
        functools.partial(kernel, geometry),
        out_shape=jax.ShapeDtypeStruct((trials, span), jnp.float32),
        in_specs=[pl.BlockSpec(memory_space=pl.ANY)] * 4,
        out_specs=pl.BlockSpec(memory_space=pltpu.VMEM),
        scratch_shapes=[
            pltpu.VMEM((channels, (own + 1) * LANES), jnp.bfloat16),
            pltpu.VMEM((1, channels), jnp.float32),
            pltpu.VMEM(local_delays.shape, jnp.int32),
            pltpu.VMEM(cross_delays.shape, jnp.int32),
            pltpu.VMEM((channels, (own + 1) * LANES), jnp.float32),
            pltpu.VMEM((local_levels, channels, LANES), jnp.int32),
            pltpu.VMEM((max(cross_levels, 1), trials, LANES), jnp.int32),
            pltpu.VMEM((phases, trials, LANES), jnp.int32),
            pltpu.VMEM((channels, frame), jnp.float32),
            pltpu.VMEM((trials, frame), jnp.float32),
            pltpu.VMEM((trials, width), jnp.float32),
            pltpu.VMEM((phases, trials, width), jnp.float32),
            pltpu.VMEM((phases, 3, trials, width), jnp.float32),
            pltpu.SemaphoreType.DMA((4,)),
            pltpu.SemaphoreType.DMA((2, row_tiles)),
            pltpu.SemaphoreType.DMA((2, row_tiles)),
            pltpu.SemaphoreType.DMA((phases,)),
            pltpu.SemaphoreType.DMA((phases,)),
            pltpu.SemaphoreType.DMA((phases, 3, row_tiles)),
            pltpu.SemaphoreType.DMA((phases, 3, row_tiles)),
        ],
        compiler_params=pltpu.CompilerParams(collective_id=0, has_side_effects=True),
    )(filterbank, bandpass.reshape(1, channels), local_delays, cross_delays)


def solution(mesh):
    return jax.shard_map(
        shards,
        mesh=mesh,
        in_specs=(P(("beam", "sub"), "tm"), P(("beam", "sub")), P(None, "sub"), P(None, "sub")),
        out_specs=P(("beam", "sub"), "tm"),
        check_vma=False,
    )
```

```python
import functools
import math

import jax
import jax.numpy as jnp
from jax import lax
from jax.experimental import pallas as pl
from jax.experimental.pallas import tpu as pltpu
from jax.sharding import PartitionSpec as P

MESH = pl.DeviceIdType.MESH
LANES = 128
SUB = 8
HALF = 15
WINDOW = 31.0


def tiles_of(columns):
    return -(-columns // LANES)


def delayed(tiles, delay, lane, count):
    tiles = tiles[max(0, len(tiles) - count - 1) :]
    source = (lane - delay) & (LANES - 1)
    keep = lane >= delay
    turned = [jnp.take_along_axis(t, source, axis=1, mode="promise_in_bounds") for t in tiles]
    if len(turned) == count:
        turned = [jnp.zeros_like(turned[0])] + turned
    return [jnp.where(keep, turned[k + 1], turned[k]) for k in range(count)]


def merged_right(lower, upper, delay, lane, count):
    source = (lane - delay) & (LANES - 1)
    keep = lane >= delay
    turned = [jnp.take_along_axis(t, source, axis=1, mode="promise_in_bounds") for t in upper]
    zero = jnp.zeros_like(turned[0])
    made = []
    for k in range(count):
        here = turned[k] if k < len(turned) else zero
        left = turned[k - 1] if k else zero
        moved = jnp.where(keep, here, left)
        made.append(lower[k] + moved if k < len(lower) else moved)
    return made


def paired(mine, theirs, on_top, delay, lane, count):
    lower = [jnp.where(on_top, t, m) for t, m in zip(theirs, mine)]
    upper = [jnp.where(on_top, m, t) for t, m in zip(theirs, mine)]
    moved = delayed(upper, delay, lane, count)
    return [a + b for a, b in zip(lower[len(lower) - count :], moved)]


def phases_of(cross_levels):
    phases = []
    for level in range(0, cross_levels, 2):
        one = 1 << level
        phases.append((level, (one, 2 * one, 3 * one) if level + 1 < cross_levels else (one,)))
    return phases


def kernel(
    geometry,
    fb_hbm, bp_hbm, ld_hbm, cd_hbm,
    out_ref,
    fpad, bp_v, ld_v, cd_v, x0, delay_l, delay_c, delay_far, plane, edge_sent, edge_got, sent, got,
    load_sem, edge_send, edge_recv, far_send, far_recv, cross_send, cross_recv,
):
    channels, span, local_levels, cross_levels, trials, shift_max, norm = geometry
    own = span // LANES
    before = tiles_of(cross_levels * shift_max)
    width = before + own
    growth = trials.bit_length() - 1
    row_tiles = trials // SUB
    tm = lax.axis_index("tm")
    sub = lax.axis_index("sub")
    other = 1 - tm
    phases = phases_of(cross_levels)

    barrier = pltpu.get_barrier_semaphore()
    pl.semaphore_signal(barrier, inc=1, device_id={"tm": other}, device_id_type=MESH)
    partners = 1
    for level, masks in phases:
        for mask in masks:
            pl.semaphore_signal(barrier, inc=1, device_id={"sub": sub ^ mask}, device_id_type=MESH)
            partners += 1

    counts = [tiles_of(span + HALF + (m + 1) * shift_max) for m in range(local_levels)]
    start = own + 1
    loads = [
        pltpu.make_async_copy(ld_hbm, ld_v, load_sem.at[0]),
        pltpu.make_async_copy(cd_hbm, cd_v, load_sem.at[1]),
        pltpu.make_async_copy(bp_hbm, bp_v, load_sem.at[2]),
        pltpu.make_async_copy(
            fb_hbm, fpad.at[:, pl.ds(pl.multiple_of(tm * LANES, LANES), span)], load_sem.at[3]
        ),
    ]
    for load in loads:
        load.start()

    @pl.when(tm == 0)
    def _():
        fpad[:, span : start * LANES] = jnp.zeros((channels, LANES), fpad.dtype)
        edge_got[:, : (width - 1) * LANES] = jnp.zeros((trials, (width - 1) * LANES), jnp.float32)

    edge_tiles = counts[-1] - own + before

    @pl.when(tm == 1)
    def _():
        fpad[:, :LANES] = jnp.zeros((channels, LANES), fpad.dtype)
        if edge_tiles < width:
            edge_got[:, edge_tiles * LANES :] = jnp.zeros((trials, (width - edge_tiles) * LANES), jnp.float32)

    for load in loads[:3]:
        load.wait()
    ones = jnp.ones((channels, LANES), jnp.float32).astype(jnp.bfloat16)
    row_at = lax.broadcasted_iota(jnp.int32, (channels, channels), 0)
    col_at = lax.broadcasted_iota(jnp.int32, (channels, channels), 1)
    diagonal = row_at == col_at
    rows = channels
    for level in range(local_levels):
        if level >= growth:
            rows //= 2
        spread = jnp.where(diagonal[:rows], ld_v[level : level + 1, :].astype(jnp.float32), 0.0)
        spread = jnp.dot(spread.astype(jnp.bfloat16), ones, preferred_element_type=jnp.float32)
        delay_l[level, :rows, :] = spread.astype(jnp.int32)
    for level in range(cross_levels):
        spread = jnp.where(diagonal[:trials, :trials], cd_v[level : level + 1, :].astype(jnp.float32), 0.0)
        spread = jnp.dot(spread.astype(jnp.bfloat16), ones[:trials], preferred_element_type=jnp.float32)
        delay_c[level] = spread.astype(jnp.int32)
    gain = jnp.dot(
        jnp.where(diagonal, bp_v[...], 0.0), jnp.ones((channels, LANES), jnp.float32),
        precision=lax.Precision.HIGHEST, preferred_element_type=jnp.float32,
    )
    band_row = lax.broadcasted_iota(jnp.int32, (3 * LANES, LANES), 0)
    band_col = lax.broadcasted_iota(jnp.int32, (3 * LANES, LANES), 1)
    apart = band_row - LANES - band_col
    band = jnp.where((apart >= -HALF) & (apart <= HALF), 1.0, 0.0).astype(jnp.bfloat16)

    loads[3].wait()
    for k in range(start):
        low, high = max(k - 1, 0), min(k + 2, start)
        total = jnp.dot(
            fpad[:, low * LANES : high * LANES], band[(low - k + 1) * LANES : (high - k + 1) * LANES],
            preferred_element_type=jnp.float32,
        )
        centre = fpad[:, k * LANES : (k + 1) * LANES].astype(jnp.float32)
        x0[:, k * LANES : (k + 1) * LANES] = gain * (centre - total / WINDOW)

    lane = lax.broadcasted_iota(jnp.int32, (SUB, LANES), 1)
    sublane = lax.broadcasted_iota(jnp.int32, (SUB, LANES), 0)

    def block(at, carry):
        base = at * trials
        current = []
        for r in range(row_tiles):
            here = pl.ds(pl.multiple_of(base + r * SUB, SUB), SUB)
            current.append([x0[here, k * LANES : (k + 1) * LANES] for k in range(start)])
        for level in range(growth):
            count, step = counts[level], 1 << level
            following = []
            for r in range(row_tiles):
                delay = delay_l[level, pl.ds(pl.multiple_of(base + r * SUB, SUB), SUB), :]
                if step < SUB:
                    is_upper = (sublane & step) != 0
                    lower, upper = [], []
                    for t in current[r]:
                        down = pltpu.roll(t, step, 0)
                        up = down if 2 * step == SUB else pltpu.roll(t, SUB - step, 0)
                        lower.append(jnp.where(is_upper, down, t))
                        upper.append(jnp.where(is_upper, t, up))
                else:
                    apart = step // SUB
                    lower, upper = current[r & ~apart], current[r | apart]
                following.append(merged_right(lower, upper, delay, lane, count))
            current = following
        for r in range(row_tiles):
            here = pl.ds(pl.multiple_of(base + r * SUB, SUB), SUB)
            for k, t in enumerate(current[r]):
                plane[here, k * LANES : (k + 1) * LANES] = t
        return carry

    lax.fori_loop(0, channels // trials, block, 0, unroll=True)

    bands = channels // trials
    count = counts[growth - 1]
    current = [
        [[plane[(b * row_tiles + r) * SUB : (b * row_tiles + r + 1) * SUB, k * LANES : (k + 1) * LANES] for k in range(count)] for r in range(row_tiles)]
        for b in range(bands)
    ]
    for level in range(growth, local_levels):
        count = counts[level]
        bands //= 2
        following = []
        for b in range(bands):
            made = []
            for r in range(row_tiles):
                at = (b * row_tiles + r) * SUB
                delay = delay_l[level, at : at + SUB, :]
                made.append(merged_right(current[2 * b][r], current[2 * b + 1][r], delay, lane, count))
            following.append(made)
        current = following
    frame = current[0]

    for r in range(row_tiles):
        for k, t in enumerate(frame[r]):
            edge_sent[r * SUB : (r + 1) * SUB, k * LANES : (k + 1) * LANES] = t
    pl.semaphore_wait(barrier, partners)

    far_copies = []
    for at, (level, masks) in enumerate(phases):
        if len(masks) > 1:
            copy = pltpu.make_async_remote_copy(
                src_ref=delay_c.at[level], dst_ref=delay_far.at[at],
                send_sem=far_send.at[at], recv_sem=far_recv.at[at],
                device_id={"sub": sub ^ masks[1]}, device_id_type=MESH,
            )
            far_copies.append(copy)

    def edges(r):
        here = pl.ds(r * SUB, SUB)
        onward = pltpu.make_async_remote_copy(
            src_ref=edge_sent.at[here, pl.ds((own - before) * LANES, edge_tiles * LANES)],
            dst_ref=edge_got.at[here, pl.ds(0, edge_tiles * LANES)],
            send_sem=edge_send.at[0, r], recv_sem=edge_recv.at[0, r],
            device_id={"tm": other}, device_id_type=MESH,
        )
        backward = pltpu.make_async_remote_copy(
            src_ref=edge_sent.at[here, pl.ds(0, LANES)],
            dst_ref=edge_got.at[here, pl.ds((width - 1) * LANES, LANES)],
            send_sem=edge_send.at[1, r], recv_sem=edge_recv.at[1, r],
            device_id={"tm": other}, device_id_type=MESH,
        )
        return onward, backward

    edge_copies = [edges(r) for r in range(row_tiles)]

    @pl.when(tm == 0)
    def _():
        for onward, backward in edge_copies:
            onward.start()

    @pl.when(tm == 1)
    def _():
        for onward, backward in edge_copies:
            backward.start()

    for copy in far_copies:
        copy.start()

    copies = []

    def send(at, r, tiles):
        skip = width - len(tiles)
        for k, t in enumerate(tiles, skip):
            sent[at, r * SUB : (r + 1) * SUB, k * LANES : (k + 1) * LANES] = t
        made = []
        for slot, mask in enumerate(phases[at][1]):
            copy = pltpu.make_async_remote_copy(
                src_ref=sent.at[at, pl.ds(r * SUB, SUB), pl.ds(skip * LANES, len(tiles) * LANES)],
                dst_ref=got.at[at, slot, pl.ds(r * SUB, SUB), pl.ds(skip * LANES, len(tiles) * LANES)],
                send_sem=cross_send.at[at, slot, r], recv_sem=cross_recv.at[at, slot, r],
                device_id={"sub": sub ^ mask}, device_id_type=MESH,
            )
            copy.start()
            made.append(copy)
        copies.extend(made)
        return made

    rows_of, flight = [], []
    for r in range(row_tiles):
        onward, backward = edge_copies[r]

        @pl.when(tm == 0)
        def _():
            backward.wait_recv()

        @pl.when(tm == 1)
        def _():
            onward.wait_recv()

        tiles = []
        for t in range(-before, own):
            k = t + before
            piece = edge_got[r * SUB : (r + 1) * SUB, k * LANES : (k + 1) * LANES]
            zero = jnp.zeros_like(piece)
            early = frame[r][t] if t >= 0 else zero
            late = frame[r][t + 1] if t >= -1 else zero
            tiles.append(piece + jnp.where(tm == 1, late, early))
        rows_of.append(tiles)
        if phases:
            flight.append(send(0, r, tiles))

    for at, (level, masks) in enumerate(phases):
        if len(masks) > 1:
            far_copies[[a for a, p in enumerate(phases) if len(p[1]) > 1].index(at)].wait_recv()
        for r in range(row_tiles):
            mine = rows_of[r]
            here = slice(r * SUB, (r + 1) * SUB)
            skip = width - len(mine)

            def landed(slot):
                flight[r][slot].wait_recv()
                return [got[at, slot, here, (k + skip) * LANES : (k + skip + 1) * LANES] for k in range(len(mine))]

            made = paired(mine, landed(0), (sub >> level) & 1 == 1, delay_c[level, here, :], lane, own + tiles_of((cross_levels - level - 1) * shift_max))
            if len(masks) > 1:
                far = paired(landed(1), landed(2), (sub >> level) & 1 == 1, delay_far[at, here, :], lane, len(made))
                made = paired(made, far, (sub >> (level + 1)) & 1 == 1, delay_c[level + 1, here, :], lane, own + tiles_of((cross_levels - level - 2) * shift_max))
            rows_of[r] = made
            if at + 1 < len(phases):
                flight[r] = send(at + 1, r, made)
    for r in range(row_tiles):
        for k, t in enumerate(rows_of[r][-own:]):
            out_ref[r * SUB : (r + 1) * SUB, k * LANES : (k + 1) * LANES] = t * norm
    for copy in copies + far_copies:
        copy.wait_send()

    @pl.when(tm == 0)
    def _():
        for onward, backward in edge_copies:
            onward.wait_send()

    @pl.when(tm == 1)
    def _():
        for onward, backward in edge_copies:
            backward.wait_send()


def shards(filterbank, bandpass, local_delays, cross_delays):
    channels, span = filterbank.shape
    shift_max = span // 16
    local_levels = local_delays.shape[0]
    cross_levels = lax.axis_size("sub").bit_length() - 1
    trials = cross_delays.shape[1]
    norm = 1.0 / math.sqrt(channels * lax.axis_size("sub"))
    own = span // LANES
    width = (own + tiles_of(cross_levels * shift_max)) * LANES
    frame = tiles_of(span + HALF + local_levels * shift_max) * LANES
    phases = max(len(phases_of(cross_levels)), 1)
    row_tiles = trials // SUB
    geometry = (channels, span, local_levels, cross_levels, trials, shift_max, norm)
    return pl.pallas_call(
        functools.partial(kernel, geometry),
        out_shape=jax.ShapeDtypeStruct((trials, span), jnp.float32),
        in_specs=[pl.BlockSpec(memory_space=pl.ANY)] * 4,
        out_specs=pl.BlockSpec(memory_space=pltpu.VMEM),
        scratch_shapes=[
            pltpu.VMEM((channels, (own + 1) * LANES), jnp.bfloat16),
            pltpu.VMEM((1, channels), jnp.float32),
            pltpu.VMEM(local_delays.shape, jnp.int32),
            pltpu.VMEM(cross_delays.shape, jnp.int32),
            pltpu.VMEM((channels, (own + 1) * LANES), jnp.float32),
            pltpu.VMEM((local_levels, channels, LANES), jnp.int32),
            pltpu.VMEM((max(cross_levels, 1), trials, LANES), jnp.int32),
            pltpu.VMEM((phases, trials, LANES), jnp.int32),
            pltpu.VMEM((channels, frame), jnp.float32),
            pltpu.VMEM((trials, frame), jnp.float32),
            pltpu.VMEM((trials, width), jnp.float32),
            pltpu.VMEM((phases, trials, width), jnp.float32),
            pltpu.VMEM((phases, 3, trials, width), jnp.float32),
            pltpu.SemaphoreType.DMA((4,)),
            pltpu.SemaphoreType.DMA((2, row_tiles)),
            pltpu.SemaphoreType.DMA((2, row_tiles)),
            pltpu.SemaphoreType.DMA((phases,)),
            pltpu.SemaphoreType.DMA((phases,)),
            pltpu.SemaphoreType.DMA((phases, 3, row_tiles)),
            pltpu.SemaphoreType.DMA((phases, 3, row_tiles)),
        ],
        compiler_params=pltpu.CompilerParams(collective_id=0, has_side_effects=True),
    )(filterbank, bandpass.reshape(1, channels), local_delays, cross_delays)


def solution(mesh):
    return jax.shard_map(
        shards,
        mesh=mesh,
        in_specs=(P(("beam", "sub"), "tm"), P(("beam", "sub")), P(None, "sub"), P(None, "sub")),
        out_specs=P(("beam", "sub"), "tm"),
        check_vma=False,
    )
```

```python
import functools
import math

import jax
import jax.numpy as jnp
from jax import lax
from jax.experimental import pallas as pl
from jax.experimental.pallas import tpu as pltpu
from jax.sharding import PartitionSpec as P

MESH = pl.DeviceIdType.MESH
LANES = 128
SUB = 8
HALF = 15
WINDOW = 31.0


def tiles_of(columns):
    return -(-columns // LANES)


def delayed(tiles, delay, lane, count):
    tiles = tiles[max(0, len(tiles) - count - 1) :]
    source = (lane - delay) & (LANES - 1)
    keep = lane >= delay
    turned = [jnp.take_along_axis(t, source, axis=1, mode="promise_in_bounds") for t in tiles]
    if len(turned) == count:
        turned = [jnp.zeros_like(turned[0])] + turned
    return [jnp.where(keep, turned[k + 1], turned[k]) for k in range(count)]


def merged_right(lower, upper, delay, lane, count):
    source = (lane - delay) & (LANES - 1)
    keep = lane >= delay
    turned = [jnp.take_along_axis(t, source, axis=1, mode="promise_in_bounds") for t in upper]
    zero = jnp.zeros_like(turned[0])
    made = []
    for k in range(count):
        here = turned[k] if k < len(turned) else zero
        left = turned[k - 1] if k else zero
        moved = jnp.where(keep, here, left)
        made.append(lower[k] + moved if k < len(lower) else moved)
    return made


def paired(mine, theirs, on_top, delay, lane, count):
    lower = [jnp.where(on_top, t, m) for t, m in zip(theirs, mine)]
    upper = [jnp.where(on_top, m, t) for t, m in zip(theirs, mine)]
    moved = delayed(upper, delay, lane, count)
    return [a + b for a, b in zip(lower[len(lower) - count :], moved)]


def phases_of(cross_levels):
    phases = []
    for level in range(0, cross_levels, 2):
        one = 1 << level
        phases.append((level, (one, 2 * one, 3 * one) if level + 1 < cross_levels else (one,)))
    return phases


def kernel(
    geometry,
    fb_hbm, bp_hbm, ld_hbm, cd_hbm,
    out_ref,
    fpad, bp_v, ld_v, cd_v, x0, delay_l, delay_c, delay_far, plane, edge_sent, edge_got, sent, got,
    load_sem, edge_send, edge_recv, far_send, far_recv, cross_send, cross_recv,
):
    channels, span, local_levels, cross_levels, trials, shift_max, norm = geometry
    own = span // LANES
    before = tiles_of(cross_levels * shift_max)
    width = before + own
    growth = trials.bit_length() - 1
    row_tiles = trials // SUB
    tm = lax.axis_index("tm")
    sub = lax.axis_index("sub")
    other = 1 - tm
    phases = phases_of(cross_levels)

    barrier = pltpu.get_barrier_semaphore()
    pl.semaphore_signal(barrier, inc=1, device_id={"tm": other}, device_id_type=MESH)
    partners = 1
    for level, masks in phases:
        for mask in masks:
            pl.semaphore_signal(barrier, inc=1, device_id={"sub": sub ^ mask}, device_id_type=MESH)
            partners += 1

    counts = [tiles_of(span + HALF + (m + 1) * shift_max) for m in range(local_levels)]
    start = own + 1
    loads = [
        pltpu.make_async_copy(ld_hbm, ld_v, load_sem.at[0]),
        pltpu.make_async_copy(cd_hbm, cd_v, load_sem.at[1]),
        pltpu.make_async_copy(bp_hbm, bp_v, load_sem.at[2]),
        pltpu.make_async_copy(
            fb_hbm, fpad.at[:, pl.ds(pl.multiple_of(tm * LANES, LANES), span)], load_sem.at[3]
        ),
    ]
    for load in loads:
        load.start()

    @pl.when(tm == 0)
    def _():
        fpad[:, span : start * LANES] = jnp.zeros((channels, LANES), fpad.dtype)
        edge_got[:, : (width - 1) * LANES] = jnp.zeros((trials, (width - 1) * LANES), jnp.float32)

    edge_tiles = counts[-1] - own + before

    @pl.when(tm == 1)
    def _():
        fpad[:, :LANES] = jnp.zeros((channels, LANES), fpad.dtype)
        if edge_tiles < width:
            edge_got[:, edge_tiles * LANES :] = jnp.zeros((trials, (width - edge_tiles) * LANES), jnp.float32)

    for load in loads[:3]:
        load.wait()
    ones = jnp.ones((channels, LANES), jnp.float32).astype(jnp.bfloat16)
    row_at = lax.broadcasted_iota(jnp.int32, (channels, channels), 0)
    col_at = lax.broadcasted_iota(jnp.int32, (channels, channels), 1)
    diagonal = row_at == col_at
    rows = channels
    for level in range(local_levels):
        if level >= growth:
            rows //= 2
        spread = jnp.where(diagonal[:rows], ld_v[level : level + 1, :].astype(jnp.float32), 0.0)
        spread = jnp.dot(spread.astype(jnp.bfloat16), ones, preferred_element_type=jnp.float32)
        delay_l[level, :rows, :] = spread.astype(jnp.int32)
    for level in range(cross_levels):
        spread = jnp.where(diagonal[:trials, :trials], cd_v[level : level + 1, :].astype(jnp.float32), 0.0)
        spread = jnp.dot(spread.astype(jnp.bfloat16), ones[:trials], preferred_element_type=jnp.float32)
        delay_c[level] = spread.astype(jnp.int32)
    gain = jnp.dot(
        jnp.where(diagonal, bp_v[...], 0.0), jnp.ones((channels, LANES), jnp.float32),
        precision=lax.Precision.HIGHEST, preferred_element_type=jnp.float32,
    )
    band_row = lax.broadcasted_iota(jnp.int32, (3 * LANES, LANES), 0)
    band_col = lax.broadcasted_iota(jnp.int32, (3 * LANES, LANES), 1)
    apart = band_row - LANES - band_col
    band = jnp.where((apart >= -HALF) & (apart <= HALF), 1.0, 0.0).astype(jnp.bfloat16)

    loads[3].wait()
    for k in range(start):
        low, high = max(k - 1, 0), min(k + 2, start)
        total = jnp.dot(
            fpad[:, low * LANES : high * LANES], band[(low - k + 1) * LANES : (high - k + 1) * LANES],
            preferred_element_type=jnp.float32,
        )
        centre = fpad[:, k * LANES : (k + 1) * LANES].astype(jnp.float32)
        x0[:, k * LANES : (k + 1) * LANES] = gain * (centre - total / WINDOW)

    lane = lax.broadcasted_iota(jnp.int32, (SUB, LANES), 1)
    sublane = lax.broadcasted_iota(jnp.int32, (SUB, LANES), 0)

    def block(at, carry):
        base = at * trials
        current = []
        for r in range(row_tiles):
            here = pl.ds(pl.multiple_of(base + r * SUB, SUB), SUB)
            current.append([x0[here, k * LANES : (k + 1) * LANES] for k in range(start)])
        for level in range(growth):
            count, step = counts[level], 1 << level
            following = []
            for r in range(row_tiles):
                delay = delay_l[level, pl.ds(pl.multiple_of(base + r * SUB, SUB), SUB), :]
                if step < SUB:
                    is_upper = (sublane & step) != 0
                    lower, upper = [], []
                    for t in current[r]:
                        down = pltpu.roll(t, step, 0)
                        up = down if 2 * step == SUB else pltpu.roll(t, SUB - step, 0)
                        lower.append(jnp.where(is_upper, down, t))
                        upper.append(jnp.where(is_upper, t, up))
                else:
                    apart = step // SUB
                    lower, upper = current[r & ~apart], current[r | apart]
                following.append(merged_right(lower, upper, delay, lane, count))
            current = following
        for r in range(row_tiles):
            here = pl.ds(pl.multiple_of(base + r * SUB, SUB), SUB)
            for k, t in enumerate(current[r]):
                plane[here, k * LANES : (k + 1) * LANES] = t
        return carry

    lax.fori_loop(0, channels // trials, block, 0, unroll=True)

    bands = channels // trials
    count = counts[growth - 1]
    current = [
        [[plane[(b * row_tiles + r) * SUB : (b * row_tiles + r + 1) * SUB, k * LANES : (k + 1) * LANES] for k in range(count)] for r in range(row_tiles)]
        for b in range(bands)
    ]
    for level in range(growth, local_levels):
        count = counts[level]
        bands //= 2
        following = []
        for b in range(bands):
            made = []
            for r in range(row_tiles):
                at = (b * row_tiles + r) * SUB
                delay = delay_l[level, at : at + SUB, :]
                made.append(merged_right(current[2 * b][r], current[2 * b + 1][r], delay, lane, count))
            following.append(made)
        current = following
    frame = current[0]

    for r in range(row_tiles):
        for k, t in enumerate(frame[r]):
            edge_sent[r * SUB : (r + 1) * SUB, k * LANES : (k + 1) * LANES] = t
    pl.semaphore_wait(barrier, partners)

    far_copies = []
    for at, (level, masks) in enumerate(phases):
        if len(masks) > 1:
            copy = pltpu.make_async_remote_copy(
                src_ref=delay_c.at[level], dst_ref=delay_far.at[at],
                send_sem=far_send.at[at], recv_sem=far_recv.at[at],
                device_id={"sub": sub ^ masks[1]}, device_id_type=MESH,
            )
            far_copies.append(copy)

    def edges(r):
        here = pl.ds(r * SUB, SUB)
        onward = pltpu.make_async_remote_copy(
            src_ref=edge_sent.at[here, pl.ds((own - before) * LANES, edge_tiles * LANES)],
            dst_ref=edge_got.at[here, pl.ds(0, edge_tiles * LANES)],
            send_sem=edge_send.at[0, r], recv_sem=edge_recv.at[0, r],
            device_id={"tm": other}, device_id_type=MESH,
        )
        backward = pltpu.make_async_remote_copy(
            src_ref=edge_sent.at[here, pl.ds(0, LANES)],
            dst_ref=edge_got.at[here, pl.ds((width - 1) * LANES, LANES)],
            send_sem=edge_send.at[1, r], recv_sem=edge_recv.at[1, r],
            device_id={"tm": other}, device_id_type=MESH,
        )
        return onward, backward

    edge_copies = [edges(r) for r in range(row_tiles)]

    @pl.when(tm == 0)
    def _():
        for onward, backward in edge_copies:
            onward.start()

    @pl.when(tm == 1)
    def _():
        for onward, backward in edge_copies:
            backward.start()

    for copy in far_copies:
        copy.start()

    copies = []

    def send(at, r, tiles):
        skip = width - len(tiles)
        for k, t in enumerate(tiles, skip):
            sent[at, r * SUB : (r + 1) * SUB, k * LANES : (k + 1) * LANES] = t
        made = []
        for slot, mask in enumerate(phases[at][1]):
            copy = pltpu.make_async_remote_copy(
                src_ref=sent.at[at, pl.ds(r * SUB, SUB), pl.ds(skip * LANES, len(tiles) * LANES)],
                dst_ref=got.at[at, slot, pl.ds(r * SUB, SUB), pl.ds(skip * LANES, len(tiles) * LANES)],
                send_sem=cross_send.at[at, slot, r], recv_sem=cross_recv.at[at, slot, r],
                device_id={"sub": sub ^ mask}, device_id_type=MESH,
            )
            copy.start()
            made.append(copy)
        copies.extend(made)
        return made

    rows_of, flight = [], []
    for r in range(row_tiles):
        onward, backward = edge_copies[r]

        @pl.when(tm == 0)
        def _():
            backward.wait_recv()

        @pl.when(tm == 1)
        def _():
            onward.wait_recv()

        tiles = []
        for t in range(-before, own):
            k = t + before
            piece = edge_got[r * SUB : (r + 1) * SUB, k * LANES : (k + 1) * LANES]
            zero = jnp.zeros_like(piece)
            early = frame[r][t] if t >= 0 else zero
            late = frame[r][t + 1] if t >= -1 else zero
            tiles.append(piece + jnp.where(tm == 1, late, early))
        rows_of.append(tiles)
        if phases:
            flight.append(send(0, r, tiles))

    for at, (level, masks) in enumerate(phases):
        if len(masks) > 1:
            far_copies[[a for a, p in enumerate(phases) if len(p[1]) > 1].index(at)].wait_recv()
        for r in range(row_tiles):
            mine = rows_of[r]
            here = slice(r * SUB, (r + 1) * SUB)
            skip = width - len(mine)

            def landed(slot):
                flight[r][slot].wait_recv()
                return [got[at, slot, here, (k + skip) * LANES : (k + skip + 1) * LANES] for k in range(len(mine))]

            made = paired(mine, landed(0), (sub >> level) & 1 == 1, delay_c[level, here, :], lane, own + tiles_of((cross_levels - level - 1) * shift_max))
            if len(masks) > 1:
                far = paired(landed(1), landed(2), (sub >> level) & 1 == 1, delay_far[at, here, :], lane, len(made))
                made = paired(made, far, (sub >> (level + 1)) & 1 == 1, delay_c[level + 1, here, :], lane, own + tiles_of((cross_levels - level - 2) * shift_max))
            rows_of[r] = made
            if at + 1 < len(phases):
                flight[r] = send(at + 1, r, made)
    for r in range(row_tiles):
        for k, t in enumerate(rows_of[r][-own:]):
            out_ref[r * SUB : (r + 1) * SUB, k * LANES : (k + 1) * LANES] = t * norm
    for copy in copies + far_copies:
        copy.wait_send()

    @pl.when(tm == 0)
    def _():
        for onward, backward in edge_copies:
            onward.wait_send()

    @pl.when(tm == 1)
    def _():
        for onward, backward in edge_copies:
            backward.wait_send()


def shards(filterbank, bandpass, local_delays, cross_delays):
    channels, span = filterbank.shape
    shift_max = span // 16
    local_levels = local_delays.shape[0]
    cross_levels = lax.axis_size("sub").bit_length() - 1
    trials = cross_delays.shape[1]
    norm = 1.0 / math.sqrt(channels * lax.axis_size("sub"))
    own = span // LANES
    width = (own + tiles_of(cross_levels * shift_max)) * LANES
    frame = tiles_of(span + HALF + local_levels * shift_max) * LANES
    phases = max(len(phases_of(cross_levels)), 1)
    row_tiles = trials // SUB
    geometry = (channels, span, local_levels, cross_levels, trials, shift_max, norm)
    return pl.pallas_call(
        functools.partial(kernel, geometry),
        out_shape=pltpu.VMEM((trials, span), jnp.float32),
        in_specs=[pl.BlockSpec(memory_space=pl.ANY)] * 4,
        out_specs=pl.BlockSpec(memory_space=pltpu.VMEM),
        scratch_shapes=[
            pltpu.VMEM((channels, (own + 1) * LANES), jnp.bfloat16),
            pltpu.VMEM((1, channels), jnp.float32),
            pltpu.VMEM(local_delays.shape, jnp.int32),
            pltpu.VMEM(cross_delays.shape, jnp.int32),
            pltpu.VMEM((channels, (own + 1) * LANES), jnp.float32),
            pltpu.VMEM((local_levels, channels, LANES), jnp.int32),
            pltpu.VMEM((max(cross_levels, 1), trials, LANES), jnp.int32),
            pltpu.VMEM((phases, trials, LANES), jnp.int32),
            pltpu.VMEM((channels, frame), jnp.float32),
            pltpu.VMEM((trials, frame), jnp.float32),
            pltpu.VMEM((trials, width), jnp.float32),
            pltpu.VMEM((phases, trials, width), jnp.float32),
            pltpu.VMEM((phases, 3, trials, width), jnp.float32),
            pltpu.SemaphoreType.DMA((4,)),
            pltpu.SemaphoreType.DMA((2, row_tiles)),
            pltpu.SemaphoreType.DMA((2, row_tiles)),
            pltpu.SemaphoreType.DMA((phases,)),
            pltpu.SemaphoreType.DMA((phases,)),
            pltpu.SemaphoreType.DMA((phases, 3, row_tiles)),
            pltpu.SemaphoreType.DMA((phases, 3, row_tiles)),
        ],
        compiler_params=pltpu.CompilerParams(collective_id=0, has_side_effects=True),
    )(filterbank, bandpass.reshape(1, channels), local_delays, cross_delays)


def solution(mesh):
    return jax.shard_map(
        shards,
        mesh=mesh,
        in_specs=(P(("beam", "sub"), "tm"), P(("beam", "sub")), P(None, "sub"), P(None, "sub")),
        out_specs=P(("beam", "sub"), "tm"),
        check_vma=False,
    )
```

```python
import functools
import math

import jax
import jax.numpy as jnp
from jax import lax
from jax.experimental import pallas as pl
from jax.experimental.pallas import tpu as pltpu
from jax.sharding import PartitionSpec as P

MESH = pl.DeviceIdType.MESH
LANES = 128
SUB = 8
HALF = 15
WINDOW = 31.0


def tiles_of(columns):
    return -(-columns // LANES)


def delayed(tiles, delay, lane, count):
    tiles = tiles[max(0, len(tiles) - count - 1) :]
    source = (lane - delay) & (LANES - 1)
    keep = lane >= delay
    turned = [jnp.take_along_axis(t, source, axis=1, mode="promise_in_bounds") for t in tiles]
    if len(turned) == count:
        turned = [jnp.zeros_like(turned[0])] + turned
    return [jnp.where(keep, turned[k + 1], turned[k]) for k in range(count)]


def merged_right(lower, upper, delay, lane, count):
    source = (lane - delay) & (LANES - 1)
    keep = lane >= delay
    turned = [jnp.take_along_axis(t, source, axis=1, mode="promise_in_bounds") for t in upper]
    zero = jnp.zeros_like(turned[0])
    made = []
    for k in range(count):
        here = turned[k] if k < len(turned) else zero
        left = turned[k - 1] if k else zero
        moved = jnp.where(keep, here, left)
        made.append(lower[k] + moved if k < len(lower) else moved)
    return made


def paired(mine, theirs, on_top, delay, lane, count):
    lower = [jnp.where(on_top, t, m) for t, m in zip(theirs, mine)]
    upper = [jnp.where(on_top, m, t) for t, m in zip(theirs, mine)]
    moved = delayed(upper, delay, lane, count)
    return [a + b for a, b in zip(lower[len(lower) - count :], moved)]


def phases_of(cross_levels):
    phases = []
    for level in range(0, cross_levels, 2):
        one = 1 << level
        phases.append((level, (one, 2 * one, 3 * one) if level + 1 < cross_levels else (one,)))
    return phases


def kernel(
    geometry,
    fb_hbm, bp_hbm, ld_hbm, cd_hbm,
    out_ref,
    fpad, bp_v, ld_v, cd_v, x0, delay_l, delay_c, delay_far, plane, edge_sent, edge_got, sent, got,
    load_sem, edge_send, edge_recv, far_send, far_recv, cross_send, cross_recv,
):
    channels, span, local_levels, cross_levels, trials, shift_max, norm = geometry
    own = span // LANES
    before = tiles_of(cross_levels * shift_max)
    width = before + own
    growth = trials.bit_length() - 1
    row_tiles = trials // SUB
    tm = lax.axis_index("tm")
    sub = lax.axis_index("sub")
    other = 1 - tm
    phases = phases_of(cross_levels)

    barrier = pltpu.get_barrier_semaphore()
    pl.semaphore_signal(barrier, inc=1, device_id={"tm": other}, device_id_type=MESH)
    partners = 1
    for level, masks in phases:
        for mask in masks:
            pl.semaphore_signal(barrier, inc=1, device_id={"sub": sub ^ mask}, device_id_type=MESH)
            partners += 1
    edge_masks = (0,) + (phases[0][1] if phases else ())
    for mask in edge_masks[1:]:
        pl.semaphore_signal(barrier, inc=1, device_id={"sub": sub ^ mask, "tm": other}, device_id_type=MESH)
        partners += 1

    counts = [tiles_of(span + HALF + (m + 1) * shift_max) for m in range(local_levels)]
    start = own + 1
    loads = [
        pltpu.make_async_copy(ld_hbm, ld_v, load_sem.at[0]),
        pltpu.make_async_copy(cd_hbm, cd_v, load_sem.at[1]),
        pltpu.make_async_copy(bp_hbm, bp_v, load_sem.at[2]),
        pltpu.make_async_copy(
            fb_hbm, fpad.at[:, pl.ds(pl.multiple_of(tm * LANES, LANES), span)], load_sem.at[3]
        ),
    ]
    for load in loads:
        load.start()

    @pl.when(tm == 0)
    def _():
        fpad[:, span : start * LANES] = jnp.zeros((channels, LANES), fpad.dtype)
        for slot in range(len(edge_masks)):
            edge_got[slot, :, : (width - 1) * LANES] = jnp.zeros((trials, (width - 1) * LANES), jnp.float32)

    edge_tiles = counts[-1] - own + before

    @pl.when(tm == 1)
    def _():
        fpad[:, :LANES] = jnp.zeros((channels, LANES), fpad.dtype)
        if edge_tiles < width:
            for slot in range(len(edge_masks)):
                edge_got[slot, :, edge_tiles * LANES :] = jnp.zeros((trials, (width - edge_tiles) * LANES), jnp.float32)

    for load in loads[:3]:
        load.wait()
    ones = jnp.ones((channels, LANES), jnp.float32).astype(jnp.bfloat16)
    row_at = lax.broadcasted_iota(jnp.int32, (channels, channels), 0)
    col_at = lax.broadcasted_iota(jnp.int32, (channels, channels), 1)
    diagonal = row_at == col_at
    rows = channels
    for level in range(local_levels):
        if level >= growth:
            rows //= 2
        spread = jnp.where(diagonal[:rows], ld_v[level : level + 1, :].astype(jnp.float32), 0.0)
        spread = jnp.dot(spread.astype(jnp.bfloat16), ones, preferred_element_type=jnp.float32)
        delay_l[level, :rows, :] = spread.astype(jnp.int32)
    for level in range(cross_levels):
        spread = jnp.where(diagonal[:trials, :trials], cd_v[level : level + 1, :].astype(jnp.float32), 0.0)
        spread = jnp.dot(spread.astype(jnp.bfloat16), ones[:trials], preferred_element_type=jnp.float32)
        delay_c[level] = spread.astype(jnp.int32)
    gain = jnp.dot(
        jnp.where(diagonal, bp_v[...], 0.0), jnp.ones((channels, LANES), jnp.float32),
        precision=lax.Precision.HIGHEST, preferred_element_type=jnp.float32,
    )
    band_row = lax.broadcasted_iota(jnp.int32, (3 * LANES, LANES), 0)
    band_col = lax.broadcasted_iota(jnp.int32, (3 * LANES, LANES), 1)
    apart = band_row - LANES - band_col
    band = jnp.where((apart >= -HALF) & (apart <= HALF), 1.0, 0.0).astype(jnp.bfloat16)

    loads[3].wait()
    for k in range(start):
        low, high = max(k - 1, 0), min(k + 2, start)
        total = jnp.dot(
            fpad[:, low * LANES : high * LANES], band[(low - k + 1) * LANES : (high - k + 1) * LANES],
            preferred_element_type=jnp.float32,
        )
        centre = fpad[:, k * LANES : (k + 1) * LANES].astype(jnp.float32)
        x0[:, k * LANES : (k + 1) * LANES] = gain * (centre - total / WINDOW)

    lane = lax.broadcasted_iota(jnp.int32, (SUB, LANES), 1)
    sublane = lax.broadcasted_iota(jnp.int32, (SUB, LANES), 0)

    def block(at, carry):
        base = at * trials
        current = []
        for r in range(row_tiles):
            here = pl.ds(pl.multiple_of(base + r * SUB, SUB), SUB)
            current.append([x0[here, k * LANES : (k + 1) * LANES] for k in range(start)])
        for level in range(growth):
            count, step = counts[level], 1 << level
            following = []
            for r in range(row_tiles):
                delay = delay_l[level, pl.ds(pl.multiple_of(base + r * SUB, SUB), SUB), :]
                if step < SUB:
                    is_upper = (sublane & step) != 0
                    lower, upper = [], []
                    for t in current[r]:
                        down = pltpu.roll(t, step, 0)
                        up = down if 2 * step == SUB else pltpu.roll(t, SUB - step, 0)
                        lower.append(jnp.where(is_upper, down, t))
                        upper.append(jnp.where(is_upper, t, up))
                else:
                    apart = step // SUB
                    lower, upper = current[r & ~apart], current[r | apart]
                following.append(merged_right(lower, upper, delay, lane, count))
            current = following
        for r in range(row_tiles):
            here = pl.ds(pl.multiple_of(base + r * SUB, SUB), SUB)
            for k, t in enumerate(current[r]):
                plane[here, k * LANES : (k + 1) * LANES] = t
        return carry

    lax.fori_loop(0, channels // trials, block, 0, unroll=True)

    bands = channels // trials
    count = counts[growth - 1]
    current = [
        [[plane[(b * row_tiles + r) * SUB : (b * row_tiles + r + 1) * SUB, k * LANES : (k + 1) * LANES] for k in range(count)] for r in range(row_tiles)]
        for b in range(bands)
    ]
    for level in range(growth, local_levels):
        count = counts[level]
        bands //= 2
        following = []
        for b in range(bands):
            made = []
            for r in range(row_tiles):
                at = (b * row_tiles + r) * SUB
                delay = delay_l[level, at : at + SUB, :]
                made.append(merged_right(current[2 * b][r], current[2 * b + 1][r], delay, lane, count))
            following.append(made)
        current = following
    frame = current[0]

    for r in range(row_tiles):
        for k, t in enumerate(frame[r]):
            edge_sent[r * SUB : (r + 1) * SUB, k * LANES : (k + 1) * LANES] = t
    pl.semaphore_wait(barrier, partners)

    far_copies = []
    for at, (level, masks) in enumerate(phases):
        if len(masks) > 1:
            copy = pltpu.make_async_remote_copy(
                src_ref=delay_c.at[level], dst_ref=delay_far.at[at],
                send_sem=far_send.at[at], recv_sem=far_recv.at[at],
                device_id={"sub": sub ^ masks[1]}, device_id_type=MESH,
            )
            far_copies.append(copy)

    def edges(r, slot, mask):
        here = pl.ds(r * SUB, SUB)
        target = {"sub": sub ^ mask, "tm": other} if mask else {"tm": other}
        onward = pltpu.make_async_remote_copy(
            src_ref=edge_sent.at[here, pl.ds((own - before) * LANES, edge_tiles * LANES)],
            dst_ref=edge_got.at[slot, here, pl.ds(0, edge_tiles * LANES)],
            send_sem=edge_send.at[0, slot, r], recv_sem=edge_recv.at[0, slot, r],
            device_id=target, device_id_type=MESH,
        )
        backward = pltpu.make_async_remote_copy(
            src_ref=edge_sent.at[here, pl.ds(0, LANES)],
            dst_ref=edge_got.at[slot, here, pl.ds((width - 1) * LANES, LANES)],
            send_sem=edge_send.at[1, slot, r], recv_sem=edge_recv.at[1, slot, r],
            device_id=target, device_id_type=MESH,
        )
        return onward, backward

    edge_copies = [[edges(r, slot, mask) for slot, mask in enumerate(edge_masks)] for r in range(row_tiles)]

    for copy in far_copies:
        copy.start()

    copies = []

    def send(at, r, tiles):
        skip = width - len(tiles)
        for k, t in enumerate(tiles, skip):
            sent[at, r * SUB : (r + 1) * SUB, k * LANES : (k + 1) * LANES] = t
        made = []
        for slot, mask in enumerate(phases[at][1]):
            copy = pltpu.make_async_remote_copy(
                src_ref=sent.at[at, pl.ds(r * SUB, SUB), pl.ds(skip * LANES, len(tiles) * LANES)],
                dst_ref=got.at[at, slot, pl.ds(r * SUB, SUB), pl.ds(skip * LANES, len(tiles) * LANES)],
                send_sem=cross_send.at[at, slot, r], recv_sem=cross_recv.at[at, slot, r],
                device_id={"sub": sub ^ mask}, device_id_type=MESH,
            )
            copy.start()
            made.append(copy)
        copies.extend(made)
        return made

    def with_edge(r, slot, tiles):
        onward, backward = edge_copies[r][slot]

        @pl.when(tm == 0)
        def _():
            backward.wait_recv()

        @pl.when(tm == 1)
        def _():
            onward.wait_recv()

        return [t + edge_got[slot, r * SUB : (r + 1) * SUB, k * LANES : (k + 1) * LANES] for k, t in enumerate(tiles)]

    rows_of, flight = [], []
    for r in range(row_tiles):
        tiles = []
        for t in range(-before, own):
            zero = jnp.zeros_like(frame[r][0])
            early = frame[r][t] if t >= 0 else zero
            late = frame[r][t + 1] if t >= -1 else zero
            tiles.append(jnp.where(tm == 1, late, early))
        rows_of.append(tiles)
        if phases:
            flight.append(send(0, r, tiles))

        @pl.when(tm == 0)
        def _():
            for onward, backward in edge_copies[r]:
                onward.start()

        @pl.when(tm == 1)
        def _():
            for onward, backward in edge_copies[r]:
                backward.start()

    for r in range(row_tiles):
        rows_of[r] = with_edge(r, 0, rows_of[r])
    for at, (level, masks) in enumerate(phases):
        if len(masks) > 1:
            far_copies[[a for a, p in enumerate(phases) if len(p[1]) > 1].index(at)].wait_recv()
        for r in range(row_tiles):
            mine = rows_of[r]
            here = slice(r * SUB, (r + 1) * SUB)
            skip = width - len(mine)

            def landed(slot):
                flight[r][slot].wait_recv()
                tiles = [got[at, slot, here, (k + skip) * LANES : (k + skip + 1) * LANES] for k in range(len(mine))]
                return tiles if at else with_edge(r, slot + 1, tiles)

            made = paired(mine, landed(0), (sub >> level) & 1 == 1, delay_c[level, here, :], lane, own + tiles_of((cross_levels - level - 1) * shift_max))
            if len(masks) > 1:
                far = paired(landed(1), landed(2), (sub >> level) & 1 == 1, delay_far[at, here, :], lane, len(made))
                made = paired(made, far, (sub >> (level + 1)) & 1 == 1, delay_c[level + 1, here, :], lane, own + tiles_of((cross_levels - level - 2) * shift_max))
            rows_of[r] = made
            if at + 1 < len(phases):
                flight[r] = send(at + 1, r, made)
    for r in range(row_tiles):
        for k, t in enumerate(rows_of[r][-own:]):
            out_ref[r * SUB : (r + 1) * SUB, k * LANES : (k + 1) * LANES] = t * norm
    for copy in copies + far_copies:
        copy.wait_send()

    @pl.when(tm == 0)
    def _():
        for row in edge_copies:
            for onward, backward in row:
                onward.wait_send()

    @pl.when(tm == 1)
    def _():
        for row in edge_copies:
            for onward, backward in row:
                backward.wait_send()


def shards(filterbank, bandpass, local_delays, cross_delays):
    channels, span = filterbank.shape
    shift_max = span // 16
    local_levels = local_delays.shape[0]
    cross_levels = lax.axis_size("sub").bit_length() - 1
    trials = cross_delays.shape[1]
    norm = 1.0 / math.sqrt(channels * lax.axis_size("sub"))
    own = span // LANES
    width = (own + tiles_of(cross_levels * shift_max)) * LANES
    frame = tiles_of(span + HALF + local_levels * shift_max) * LANES
    phases = max(len(phases_of(cross_levels)), 1)
    row_tiles = trials // SUB
    geometry = (channels, span, local_levels, cross_levels, trials, shift_max, norm)
    return pl.pallas_call(
        functools.partial(kernel, geometry),
        out_shape=pltpu.VMEM((trials, span), jnp.float32),
        in_specs=[pl.BlockSpec(memory_space=pl.ANY)] * 4,
        out_specs=pl.BlockSpec(memory_space=pltpu.VMEM),
        scratch_shapes=[
            pltpu.VMEM((channels, (own + 1) * LANES), jnp.bfloat16),
            pltpu.VMEM((1, channels), jnp.float32),
            pltpu.VMEM(local_delays.shape, jnp.int32),
            pltpu.VMEM(cross_delays.shape, jnp.int32),
            pltpu.VMEM((channels, (own + 1) * LANES), jnp.float32),
            pltpu.VMEM((local_levels, channels, LANES), jnp.int32),
            pltpu.VMEM((max(cross_levels, 1), trials, LANES), jnp.int32),
            pltpu.VMEM((phases, trials, LANES), jnp.int32),
            pltpu.VMEM((channels, frame), jnp.float32),
            pltpu.VMEM((trials, frame), jnp.float32),
            pltpu.VMEM((4, trials, width), jnp.float32),
            pltpu.VMEM((phases, trials, width), jnp.float32),
            pltpu.VMEM((phases, 3, trials, width), jnp.float32),
            pltpu.SemaphoreType.DMA((4,)),
            pltpu.SemaphoreType.DMA((2, 4, row_tiles)),
            pltpu.SemaphoreType.DMA((2, 4, row_tiles)),
            pltpu.SemaphoreType.DMA((phases,)),
            pltpu.SemaphoreType.DMA((phases,)),
            pltpu.SemaphoreType.DMA((phases, 3, row_tiles)),
            pltpu.SemaphoreType.DMA((phases, 3, row_tiles)),
        ],
        compiler_params=pltpu.CompilerParams(collective_id=0, has_side_effects=True),
    )(filterbank, bandpass.reshape(1, channels), local_delays, cross_delays)


def solution(mesh):
    return jax.shard_map(
        shards,
        mesh=mesh,
        in_specs=(P(("beam", "sub"), "tm"), P(("beam", "sub")), P(None, "sub"), P(None, "sub")),
        out_specs=P(("beam", "sub"), "tm"),
        check_vma=False,
    )
```
